512 devices in a mesh: depth: 32 (over x, z), rows: 16 (over y, core).
Axes of the slice: x: 4, y: 8, z: 8, core: 2. Of those that a mesh axis runs over, the one named last changes fastest.
Arguments:
- log_density: float32 [128, 2048, 2048], P('depth', 'rows'), may hold values from -6 to 6
Outputs:
- frame: float32 [4, 2048, 32, 64], P(None, 'rows', 'depth')
The draws below stay inside these ranges and needn't reach their ends.
All inputs are finite; a program needn't handle non-finite values.
Results may differ from the reference program's by a relative error of at most 0.00002.
Values sent between devices are 32-bit elements; how exact they have to be, the bound alone decides.
No kernel may reach another device: no remote copies, remote signals or barrier semaphores. Data moves between devices by JAX's collectives and lax.ppermute only.
A program may use at most 64 MiB of HBM per device.

```python
import jax
import jax.numpy as jnp
from jax import lax

W = 2048
NZ = 128
H = 2048
WB = 64
N_DEPTH = 32


def shard_levels(own_key, dims, cuts, smallest, high):
    factor_of, own = 1.0, jax.random.fold_in(own_key, 6)
    for dim, blocks in cuts:
        steps = jnp.exp(jax.random.uniform(jax.random.fold_in(own, dim), (blocks,), jnp.float32, smallest / len(cuts), high / len(cuts)))
        factor_of = factor_of * jnp.repeat(steps, dims[dim] // blocks).reshape([-1 if axis == dim else 1 for axis in range(len(dims))])
    return factor_of


def bell_draw(own_key, extent, deviation, most, cuts=(), held_as=jnp.bfloat16):
    entries = deviation * jax.random.normal(own_key, extent, jnp.float32)
    if cuts:
        entries = entries * shard_levels(own_key, extent, cuts, -0.22, 0.18)
    return jnp.clip(entries, -most, most).astype(held_as)


def setup_inputs(seed: int = 0) -> dict:
    splits = jax.random.split(jax.random.key(seed), 2)
    return {
        "log_density": bell_draw(splits[0], (NZ, H, W), 1.0, 6.0, ((0, 32), (1, 16)), jnp.float32),
    }


def shade_slab(padded, extinction, count):

    def advance(carry, index):
        accum_colour, accum_opacity = carry
        planes = lax.dynamic_slice_in_dim(padded, index, 3, 0)
        centre = planes[1, 1:-1, 1:-1]
        grad_z = 0.5 * (planes[2, 1:-1, 1:-1] - planes[0, 1:-1, 1:-1])
        grad_y = 0.5 * (planes[1, 2:, 1:-1] - planes[1, :-2, 1:-1])
        grad_x = 0.5 * (planes[1, 1:-1, 2:] - planes[1, 1:-1, :-2])
        length = jnp.sqrt(grad_z * grad_z + grad_y * grad_y + grad_x * grad_x + 1.0)
        facing = (0.6 * grad_z + 0.48 * grad_y + 0.64 * grad_x) / length
        shading = 0.3 + 0.7 * jnp.abs(facing)
        colour = jnp.stack([jax.nn.sigmoid(2.0 * centre), jnp.exp(-centre * centre), jax.nn.sigmoid(-2.0 * centre)]) * shading
        opacity = 1.0 - jnp.exp(-extinction * jnp.exp(1.5 * centre))
        weight = (1.0 - accum_opacity) * opacity
        return ((accum_colour + weight * colour, accum_opacity + weight), None)
    height = padded.shape[1] - 2
    width = padded.shape[2] - 2
    start = (jnp.zeros((3, height, width), jnp.float32), jnp.zeros((height, width), jnp.float32))
    (colour_sum, opacity_sum), _ = lax.scan(advance, start, jnp.arange(count, dtype=jnp.int32))
    return jnp.concatenate([colour_sum, opacity_sum[None]], axis=0)

def reference(log_density):
    padded = jnp.pad(log_density, 1)
    image = shade_slab(padded, 0.5 / NZ, NZ)
    return image.reshape(4, H, WB, N_DEPTH).transpose(0, 1, 3, 2)
```

```python
import functools

import jax
import jax.numpy as jnp
from jax import lax
from jax.experimental import pallas as pl
from jax.experimental.pallas import tpu as pltpu
from jax.sharding import PartitionSpec as P

RING = 8


def over(nearer, farther):
    return nearer + (1.0 - nearer[3:4]) * farther


def exact_dot(values, selection):
    high = values.astype(jnp.bfloat16)
    rest = values - high.astype(jnp.float32)
    middle = rest.astype(jnp.bfloat16)
    low = (rest - middle.astype(jnp.float32)).astype(jnp.bfloat16)
    dot = functools.partial(jnp.dot, preferred_element_type=jnp.float32)
    return dot(high, selection) + dot(middle, selection) + dot(low, selection)


def selection_matrix(width, classes):
    each = width // classes
    source = lax.broadcasted_iota(jnp.int32, (width, width), 0)
    place = lax.broadcasted_iota(jnp.int32, (width, width), 1)
    wanted = classes * lax.rem(place, each) + lax.div(place, each)
    return jnp.where(source == wanted, 1.0, 0.0).astype(jnp.bfloat16)


def split_kernel(field, out):
    width = 256
    each = width // RING
    selection = selection_matrix(width, RING)
    blocks = [
        exact_dot(field[0, :, b * width : (b + 1) * width], selection)
        for b in range(field.shape[2] // width)
    ]
    for p in range(RING):
        parts = [block[:, p * each : (p + 1) * each] for block in blocks]
        out[0, p] = jnp.concatenate(parts, axis=1)


def split_classes(field):
    slices, rows, columns = field.shape
    return pl.pallas_call(
        split_kernel,
        grid=(slices,),
        in_specs=[pl.BlockSpec((1, rows, columns), lambda i: (i, 0, 0))],
        out_specs=pl.BlockSpec((1, RING, rows, columns // RING), lambda i: (i, 0, 0, 0)),
        out_shape=jax.ShapeDtypeStruct((slices, RING, rows, columns // RING), jnp.float32),
        name="split_classes",
    )(field)


def shade_kernel(extinction, own, before, after, up, down, out):
    slices, _, rows, lanes = own.shape
    sub = lax.broadcasted_iota(jnp.int32, (8, lanes), 0)
    lane = lax.broadcasted_iota(jnp.int32, (8, lanes), 1)

    def row_block(block, carry):
        start = pl.multiple_of(block * 8, 8)
        here = pl.ds(start, 8)
        first = block == 0
        final = block == rows // 8 - 1
        row_above = pl.ds(jnp.maximum(start - 1, 0), 1)
        row_below = pl.ds(jnp.minimum(start + 8, rows - 1), 1)
        for p in range(RING):
            column = [before[p, here, :]]
            column += [own[i, p, here, :] for i in range(slices)]
            column += [after[p, here, :]]
            clear = jnp.ones((8, lanes), jnp.float32)
            red = green = blue = jnp.zeros((8, lanes), jnp.float32)
            for i in range(slices):
                s = column[i + 1]
                dz = column[i + 2] - column[i]
                k = i * RING + p
                above = jnp.where(first, up[k : k + 1, :], own[i, p, row_above, :])
                below = jnp.where(final, down[k : k + 1, :], own[i, p, row_below, :])
                above = jnp.where(sub == 0, above, pltpu.roll(s, 1, 0))
                below = jnp.where(sub == 7, below, pltpu.roll(s, 7, 0))
                dy = below - above
                if p > 0:
                    left = own[i, p - 1, here, :]
                else:
                    left = pltpu.roll(own[i, RING - 1, here, :], 1, 1)
                    left = jnp.where(lane == 0, 0.0, left)
                if p < RING - 1:
                    right = own[i, p + 1, here, :]
                else:
                    right = pltpu.roll(own[i, 0, here, :], lanes - 1, 1)
                    right = jnp.where(lane == lanes - 1, 0.0, right)
                dx = right - left
                inverse = lax.rsqrt(0.25 * (dz * dz + dy * dy + dx * dx) + 1.0)
                facing = jnp.abs(0.21 * dz + 0.168 * dy + 0.224 * dx) * inverse
                root = jnp.exp(0.5 * s)
                square = root * root
                fourth = square * square
                opacity = 1.0 - jnp.exp(-extinction * (square * root))
                weight = clear * opacity
                clear = clear - weight
                shaded = weight * (0.3 + facing)
                dark = shaded / (1.0 + fourth)
                red += dark * fourth
                green += shaded * jnp.exp(-s * s)
                blue += dark
            out[p, 0, here, :] = red
            out[p, 1, here, :] = green
            out[p, 2, here, :] = blue
            out[p, 3, here, :] = 1.0 - clear
        return carry

    lax.fori_loop(0, rows // 8, row_block, 0)


def shade(extinction, own, before, after, up, down):
    _, ring, rows, lanes = own.shape
    return pl.pallas_call(
        functools.partial(shade_kernel, extinction),
        in_specs=[pl.BlockSpec(memory_space=pltpu.VMEM)] * 5,
        out_specs=pl.BlockSpec(memory_space=pltpu.VMEM),
        out_shape=jax.ShapeDtypeStruct((ring, 4, rows, lanes), jnp.float32),
        name="shade",
    )(own, before, after, up, down)


def merge_kernel(place, left, own, right, extra_2, extra_3, extra_4, out):
    quarter = out.shape[3]
    groups = out.shape[0]
    image = over(over(left[...], own[...]), right[...])
    extra = extra_2[...] + extra_3[...] + extra_4[...]
    nearer = place[0] >= RING // 2
    near = jnp.where(nearer, extra, image)
    far = jnp.where(nearer, image, extra)
    image = over(near, far)
    selection = selection_matrix(quarter * groups, groups)
    for channel in range(4):
        sorted_row = exact_dot(image[channel], selection)
        for x in range(groups):
            out[x, channel] = sorted_row[:, x * quarter : (x + 1) * quarter]


def merge(place, left, image, right, extras, groups):
    _, channels, rows, lanes = image.shape
    step = 32 if rows % 32 == 0 else rows
    plain = pl.BlockSpec((channels, step, lanes), lambda i, place: (0, i, 0))
    chosen = pl.BlockSpec((None, channels, step, lanes), lambda i, place: (place[0], 0, i, 0))
    quarter = lanes // groups
    return pl.pallas_call(
        merge_kernel,
        grid_spec=pltpu.PrefetchScalarGridSpec(
            num_scalar_prefetch=1,
            grid=(rows // step,),
            in_specs=[plain, chosen, plain, plain, plain, plain],
            out_specs=pl.BlockSpec((groups, channels, step, quarter), lambda i, place: (0, 0, i, 0)),
        ),
        out_shape=jax.ShapeDtypeStruct((groups, channels, rows, quarter), jnp.float32),
        name="merge",
    )(place, left, image, right, *extras)


def gather_ring(image):
    depth = lax.axis_size("depth")
    index = lax.axis_index("depth")
    place = lax.rem(index, RING)
    last = depth - 1
    top = depth - RING

    def piece(p):
        return lax.dynamic_index_in_dim(image, lax.rem(p + RING, RING), 0, keepdims=False)

    left = right = None
    extras = []
    for step in range(1, 5):
        distance = 5 - step
        forward = piece(place + distance)
        backward = piece(place - distance)
        if step > 1:
            forward = over(left, forward)
            backward = over(backward, right)
            extra = jnp.where(place >= RING // 2, forward, backward)
            pairs = [(last, top + distance - 1), (0, RING - distance)]
            extras.append(lax.ppermute(extra, "depth", pairs))
        half = RING // 2
        ups = [(i, i + 1) for i in range(last) if step > 1 or i % RING < half]
        downs = [(i + 1, i) for i in range(last) if step > 1 or (i + 1) % RING >= half]
        left = lax.ppermute(forward, "depth", ups)
        right = lax.ppermute(backward, "depth", downs)
    groups = depth // RING
    quarters = merge(place[None], left, image, right, extras, groups)
    group = lax.div(index, RING)
    received = []
    for shift in range(groups):
        part = lax.dynamic_index_in_dim(quarters, lax.rem(group + shift, groups), 0, keepdims=False)
        if shift:
            pairs = [(i, (i + RING * shift) % depth) for i in range(depth)]
            part = lax.ppermute(part, "depth", pairs)
        received.append(part)
    total = late = jnp.zeros_like(received[0])
    for shift in range(groups - 1, -1, -1):
        turn = shift == group
        late = jnp.where(turn, total, late)
        total = jnp.where(turn, received[shift], over(total, received[shift]))
    return over(total, late)


def local(log_density):
    slices, rows, _ = log_density.shape
    depth = lax.axis_size("depth")
    own = split_classes(log_density)
    ups = [(i, i + 1) for i in range(depth - 1)]
    downs = [(j, i) for i, j in ups]
    before = lax.ppermute(own[slices - 1], "depth", ups)
    after = lax.ppermute(own[0], "depth", downs)
    count = lax.axis_size("rows")
    row_ups = [(i, i + 1) for i in range(count - 1)]
    row_downs = [(j, i) for i, j in row_ups]
    lanes = own.shape[3]
    up = lax.ppermute(own[:, :, rows - 1, :].reshape(slices * RING, lanes), "rows", row_ups)
    down = lax.ppermute(own[:, :, 0, :].reshape(slices * RING, lanes), "rows", row_downs)
    image = shade(0.5 / (slices * depth), own, before, after, up, down)
    return gather_ring(image)[:, :, None, :]


def solution(mesh):
    return jax.shard_map(
        local,
        mesh=mesh,
        in_specs=(P("depth", "rows", None),),
        out_specs=P(None, "rows", "depth", None),
        check_vma=False,
    )
```

```python
import functools

import jax
import jax.numpy as jnp
from jax import lax
from jax.experimental import pallas as pl
from jax.experimental.pallas import tpu as pltpu
from jax.sharding import PartitionSpec as P

RING = 8
STREAMS = 2


def over(nearer, farther):
    return nearer + (1.0 - nearer[3:4]) * farther


def exact_dot(values, selection):
    high = values.astype(jnp.bfloat16)
    rest = values - high.astype(jnp.float32)
    middle = rest.astype(jnp.bfloat16)
    low = (rest - middle.astype(jnp.float32)).astype(jnp.bfloat16)
    dot = functools.partial(jnp.dot, preferred_element_type=jnp.float32)
    return dot(high, selection) + dot(middle, selection) + dot(low, selection)


def selection_matrix(width, classes):
    each = width // classes
    source = lax.broadcasted_iota(jnp.int32, (width, width), 0)
    place = lax.broadcasted_iota(jnp.int32, (width, width), 1)
    wanted = classes * lax.rem(place, each) + lax.div(place, each)
    return jnp.where(source == wanted, 1.0, 0.0).astype(jnp.bfloat16)


def split_rows(field):
    width = 256
    each = width // RING
    selection = selection_matrix(width, RING)
    blocks = [
        exact_dot(field[:, b * width : (b + 1) * width], selection)
        for b in range(field.shape[1] // width)
    ]
    for p in range(RING):
        yield jnp.concatenate([block[:, p * each : (p + 1) * each] for block in blocks], axis=1)


def split_kernel(*refs):
    half = len(refs) // 2
    for field, out in zip(refs[:half], refs[half:]):
        for p, values in enumerate(split_rows(field[...])):
            out[p] = values


def split_classes(field, stream, rows, chosen):
    columns = field.shape[2]
    step = min(rows, 32)
    steps = rows // step

    def source(i):
        return pl.BlockSpec((None, step, columns), lambda r: (i, stream * steps + r, 0))

    lanes = columns // RING
    return pl.pallas_call(
        split_kernel,
        grid=(steps,),
        in_specs=[source(i) for i in chosen],
        out_specs=[pl.BlockSpec((RING, step, lanes), lambda r: (0, r, 0)) for _ in chosen],
        out_shape=[jax.ShapeDtypeStruct((RING, rows, lanes), jnp.float32) for _ in chosen],
        cost_estimate=pl.CostEstimate(
            flops=len(chosen) * rows * columns * 1536,
            bytes_accessed=len(chosen) * rows * columns * 8,
            transcendentals=0,
        ),
        name="split_classes",
    )(*[field] * len(chosen))


PARTS = 14


def prepare_kernel(extinction, count, *refs):
    own = refs[:count]
    up, down, out = refs[count:]
    _, rows, lanes = own[0].shape
    sub = lax.broadcasted_iota(jnp.int32, (8, lanes), 0)
    lane = lax.broadcasted_iota(jnp.int32, (8, lanes), 1)

    def row_block(block, carry):
        start = pl.multiple_of(block * 8, 8)
        here = pl.ds(start, 8)
        first = block == 0
        final = block == rows // 8 - 1
        row_above = pl.ds(jnp.maximum(start - 1, 0), 1)
        row_below = pl.ds(jnp.minimum(start + 8, rows - 1), 1)
        for p in range(RING):
            column = [field[p, here, :] for field in own]
            clear = jnp.ones((8, lanes), jnp.float32)
            red = green = blue = jnp.zeros((8, lanes), jnp.float32)
            for i, field in enumerate(own):
                s = column[i]
                k = i * RING + p
                above = jnp.where(first, up[k : k + 1, :], field[p, row_above, :])
                below = jnp.where(final, down[k : k + 1, :], field[p, row_below, :])
                above = jnp.where(sub == 0, above, pltpu.roll(s, 1, 0))
                below = jnp.where(sub == 7, below, pltpu.roll(s, 7, 0))
                dy = below - above
                if p > 0:
                    left = field[p - 1, here, :]
                else:
                    left = pltpu.roll(field[RING - 1, here, :], 1, 1)
                    left = jnp.where(lane == 0, 0.0, left)
                if p < RING - 1:
                    right = field[p + 1, here, :]
                else:
                    right = pltpu.roll(field[0, here, :], lanes - 1, 1)
                    right = jnp.where(lane == lanes - 1, 0.0, right)
                dx = right - left
                sloped = 0.168 * dy + 0.224 * dx
                squared = 0.25 * (dy * dy + dx * dx) + 1.0
                root = jnp.exp(0.5 * s)
                square = root * root
                fourth = square * square
                opacity = 1.0 - jnp.exp(-extinction * (square * root))
                weight = clear * opacity
                clear = clear - weight
                if 0 < i < count - 1:
                    dz = column[i + 1] - column[i - 1]
                    weight *= shade(dz, sloped, squared)
                dark = weight / (1.0 + fourth)
                bright = dark * fourth
                glow = weight * jnp.exp(-s * s)
                if 0 < i < count - 1:
                    red += bright
                    green += glow
                    blue += dark
                else:
                    base = 4 if i == 0 else 9
                    out[p, base, here, :] = bright
                    out[p, base + 1, here, :] = glow
                    out[p, base + 2, here, :] = dark
                    out[p, base + 3, here, :] = sloped
                    out[p, base + 4, here, :] = squared
            out[p, 0, here, :] = red
            out[p, 1, here, :] = green
            out[p, 2, here, :] = blue
            out[p, 3, here, :] = 1.0 - clear
        return carry

    lax.fori_loop(0, rows // 8, row_block, 0)


def shade(dz, sloped, squared):
    return 0.3 + jnp.abs(0.21 * dz + sloped) * lax.rsqrt(0.25 * (dz * dz) + squared)


def prepare(extinction, own, up, down):
    ring, rows, lanes = own[0].shape
    cells = ring * rows * lanes
    return pl.pallas_call(
        functools.partial(prepare_kernel, extinction, len(own)),
        in_specs=[pl.BlockSpec(memory_space=pltpu.VMEM)] * (len(own) + 2),
        out_specs=pl.BlockSpec(memory_space=pltpu.VMEM),
        out_shape=jax.ShapeDtypeStruct((ring, PARTS, rows, lanes), jnp.float32),
        cost_estimate=pl.CostEstimate(
            flops=len(own) * cells * 50, bytes_accessed=72 * cells, transcendentals=len(own) * cells * 5
        ),
        name="prepare",
    )(*own, up, down)


def slab_image(parts, second, before, inner, after):
    opening = shade(second[...] - before[...], parts[7], parts[8])
    closing = shade(after[...] - inner[...], parts[12], parts[13])
    colour = [parts[c] + opening * parts[4 + c] + closing * parts[9 + c] for c in range(3)]
    return jnp.stack(colour + [parts[3]])


def step_kernel(place, *refs):
    ahead, behind = slab_image(*refs[:5]), slab_image(*refs[5:10])
    if len(refs) == 12:
        forward, backward = refs[10:]
    else:
        left, right, forward, backward, extra = refs[10:]
        ahead = over(left[...], ahead)
        behind = over(behind, right[...])
        extra[...] = jnp.where(place[2] > 0, ahead, behind)
    forward[...] = ahead
    backward[...] = behind


def chunk_specs(k, step, lanes):
    whole = pl.BlockSpec((None, PARTS, step, lanes), lambda i, place: (place[k], 0, i, 0))
    plane = pl.BlockSpec((None, step, lanes), lambda i, place: (place[k], i, 0))
    return [whole] + [plane] * 4


def image_spec(step, lanes):
    return pl.BlockSpec((4, step, lanes), lambda i, place: (0, i, 0))


def compose(place, slab, received):
    _, rows, lanes = slab[1].shape
    step = min(rows, 32)
    image = image_spec(step, lanes)
    results = 3 if received else 2
    return pl.pallas_call(
        step_kernel,
        grid_spec=pltpu.PrefetchScalarGridSpec(
            num_scalar_prefetch=1,
            grid=(rows // step,),
            in_specs=chunk_specs(0, step, lanes) + chunk_specs(1, step, lanes) + [image] * len(received),
            out_specs=[image] * results,
        ),
        out_shape=[jax.ShapeDtypeStruct((4, rows, lanes), jnp.float32)] * results,
        cost_estimate=pl.CostEstimate(
            flops=rows * lanes * 80, bytes_accessed=rows * lanes * 220, transcendentals=rows * lanes * 4
        ),
        name="compose",
    )(place, *slab, *slab, *received)


def merge_kernel(place, parts, second, before, inner, after, left, right, *refs):
    *extras, out = refs
    quarter = out.shape[3]
    groups = out.shape[0]
    image = slab_image(parts, second, before, inner, after)
    image = over(over(left[...], image), right[...])
    extra = extras[0][...] + extras[1][...] + extras[2][...]
    nearer = place[1] > 0
    near = jnp.where(nearer, extra, image)
    far = jnp.where(nearer, image, extra)
    image = over(near, far)
    selection = selection_matrix(quarter * groups, groups)
    for channel in range(4):
        sorted_row = exact_dot(image[channel], selection)
        for x in range(groups):
            out[x, channel] = sorted_row[:, x * quarter : (x + 1) * quarter]


def merge(place, slab, left, right, extras, groups):
    _, rows, lanes = slab[1].shape
    step = min(rows, 32)
    quarter = lanes // groups
    images = [left, right, *extras]
    return pl.pallas_call(
        merge_kernel,
        grid_spec=pltpu.PrefetchScalarGridSpec(
            num_scalar_prefetch=1,
            grid=(rows // step,),
            in_specs=chunk_specs(0, step, lanes) + [image_spec(step, lanes)] * len(images),
            out_specs=pl.BlockSpec((groups, 4, step, quarter), lambda i, place: (0, 0, i, 0)),
        ),
        out_shape=jax.ShapeDtypeStruct((groups, 4, rows, quarter), jnp.float32),
        cost_estimate=pl.CostEstimate(
            flops=rows * lanes * 80, bytes_accessed=rows * lanes * 200, transcendentals=rows * lanes * 2
        ),
        name="merge",
    )(place, *slab, *images)


def gather_ring(slab):
    depth = lax.axis_size("depth")
    index = lax.axis_index("depth")
    place = lax.rem(index, RING)
    last = depth - 1
    top = depth - RING
    half = RING // 2
    upper = (place >= half).astype(jnp.int32)
    send = functools.partial(lax.ppermute, axis_name="depth")
    received = []
    extras = []
    for step in range(1, 5):
        distance = 5 - step
        chunks = [lax.rem(place + distance, RING), lax.rem(place - distance + RING, RING), upper]
        forward, backward, *extra = compose(jnp.stack(chunks), slab, received)
        ups = [(i, i + 1) for i in range(last) if step > 1 or i % RING < half]
        downs = [(i + 1, i) for i in range(last) if step > 1 or (i + 1) % RING >= half]
        received = [send(forward, perm=ups), send(backward, perm=downs)]
        if extra:
            ends = (last, top + distance - 1), (0, RING - distance)
            if step == 3:
                detour = last - RING, RING
                extra[0] = send(extra[0], perm=[(last, detour[0]), (0, detour[1])])
                ends = (detour[0], ends[0][1]), (detour[1], ends[1][1])
            extras.append(send(extra[0], perm=ends))
    groups = depth // RING
    quarters = merge(jnp.stack([place, upper]), slab, *received, extras, groups)
    group = lax.div(index, RING)
    parts = []
    for shift in range(groups):
        part = lax.dynamic_index_in_dim(quarters, lax.rem(group + shift, groups), 0, keepdims=False)
        if shift:
            part = send(part, perm=[(i, (i + RING * shift) % depth) for i in range(depth)])
        parts.append(part)
    total = late = jnp.zeros_like(parts[0])
    for shift in range(groups - 1, -1, -1):
        turn = shift == group
        late = jnp.where(turn, total, late)
        total = jnp.where(turn, parts[shift], over(total, parts[shift]))
    return over(total, late)


def neighbours(axis):
    size = lax.axis_size(axis)
    ups = [(i, i + 1) for i in range(size - 1)]
    return ups, [(j, i) for i, j in ups]


def local(log_density):
    slices, all_rows, _ = log_density.shape
    rows = all_rows // STREAMS
    streams = range(STREAMS)
    ups, downs = neighbours("depth")
    ends = [split_classes(log_density, k, rows, (0, slices - 1)) for k in streams]
    before = [lax.ppermute(final, "depth", ups) for _, final in ends]
    after = [lax.ppermute(first, "depth", downs) for first, _ in ends]
    inner = [split_classes(log_density, k, rows, range(1, slices - 1)) for k in streams]
    slabs = [[ends[k][0], *inner[k], ends[k][1]] for k in streams]

    def edge(k, row):
        return jnp.concatenate([plane[:, row] for plane in slabs[k]])

    ups, downs = neighbours("rows")
    up = [lax.ppermute(edge(STREAMS - 1, rows - 1), "rows", ups)]
    down = [lax.ppermute(edge(0, 0), "rows", downs)]
    up += [edge(k, rows - 1) for k in streams[:-1]]
    down = [edge(k, 0) for k in streams[1:]] + down
    extinction = 0.5 / (slices * lax.axis_size("depth"))
    parts = [prepare(extinction, slabs[k], up[k], down[k]) for k in streams]
    images = [
        gather_ring([parts[k], inner[k][0], before[k], inner[k][-1], after[k]]) for k in streams
    ]
    return jnp.concatenate(images, axis=1)[:, :, None, :]


def solution(mesh):
    return jax.shard_map(
        local,
        mesh=mesh,
        in_specs=(P("depth", "rows", None),),
        out_specs=P(None, "rows", "depth", None),
        check_vma=False,
    )
```

```python
import functools

import jax
import jax.numpy as jnp
from jax import lax
from jax.experimental import pallas as pl
from jax.experimental.pallas import tpu as pltpu
from jax.sharding import PartitionSpec as P

RING = 8


def over(nearer, farther):
    return nearer + (1.0 - nearer[3:4]) * farther


def thirds(values):
    high = values.astype(jnp.bfloat16)
    rest = values - high.astype(jnp.float32)
    middle = rest.astype(jnp.bfloat16)
    low = (rest - middle.astype(jnp.float32)).astype(jnp.bfloat16)
    return jnp.concatenate([high, middle, low], axis=1)


def selection_matrix(width, classes):
    each = width // classes
    source = lax.broadcasted_iota(jnp.int32, (width, width), 0)
    column = lax.broadcasted_iota(jnp.int32, (width, width), 1)
    wanted = classes * (column & (each - 1)) + (column >> (each.bit_length() - 1))
    selection = jnp.where(source == wanted, 1.0, 0.0).astype(jnp.bfloat16)
    return jnp.concatenate([selection] * 3, axis=0)


def params(mebibytes):
    return pltpu.CompilerParams(vmem_limit_bytes=mebibytes * 2**20)


def split_kernel(*refs):
    *refs, selection = refs
    count = len(refs) // 3
    width = selection.shape[1]
    each = width // RING

    @pl.when(pl.program_id(0) == 0)
    def _():
        selection[...] = selection_matrix(width, RING)

    for field, out, edge in zip(refs[:count], refs[count : 2 * count], refs[2 * count :]):
        rows, columns = field.shape
        groups = range(columns // width)
        stacked = [thirds(field[:, b * width : (b + 1) * width]) for b in groups]
        sorted_rows = jnp.dot(
            jnp.concatenate(stacked, axis=0), selection[...], preferred_element_type=jnp.float32
        )
        blocks = [sorted_rows[b * rows : (b + 1) * rows] for b in groups]
        for p in range(RING):
            parts = [block[:, p * each : (p + 1) * each] for block in blocks]
            values = jnp.concatenate(parts, axis=1)
            out[p] = values

            @pl.when(pl.program_id(0) == 0)
            def _(values=values, edge=edge, p=p):
                edge[0, p : p + 1] = values[:1]

            @pl.when(pl.program_id(0) == pl.num_programs(0) - 1)
            def _(values=values, edge=edge, p=p):
                edge[1, p : p + 1] = values[rows - 1 :]


def split_classes(field, chosen):
    _, rows, columns = field.shape
    step = min(rows, 64)
    lanes = columns // RING

    def source(i):
        return pl.BlockSpec((None, step, columns), lambda r: (i, r, 0))

    return pl.pallas_call(
        split_kernel,
        grid=(rows // step,),
        in_specs=[source(i) for i in chosen],
        out_specs=[pl.BlockSpec((RING, step, lanes), lambda r: (0, r, 0)) for _ in chosen]
        + [pl.BlockSpec((2, RING, lanes), lambda r: (0, 0, 0)) for _ in chosen],
        out_shape=[jax.ShapeDtypeStruct((RING, rows, lanes), jnp.float32) for _ in chosen]
        + [jax.ShapeDtypeStruct((2, RING, lanes), jnp.float32) for _ in chosen],
        scratch_shapes=[pltpu.VMEM((768, 256), jnp.bfloat16)],
        compiler_params=params(24),
        cost_estimate=pl.CostEstimate(
            flops=len(chosen) * rows * columns * 1536,
            bytes_accessed=len(chosen) * rows * columns * 8,
            transcendentals=0,
        ),
        name="split_classes",
    )(*[field] * len(chosen))


PARTS = 14


def prepare_kernel(extinction, count, *refs):
    own = refs[:count]
    up, down, out = refs[count:]
    _, rows, lanes = own[0].shape
    sub = lax.broadcasted_iota(jnp.int32, (8, lanes), 0)
    lane = lax.broadcasted_iota(jnp.int32, (8, lanes), 1)

    def row_block(block, carry):
        start = pl.multiple_of(block * 8, 8)
        here = pl.ds(start, 8)
        first = block == 0
        final = block == rows // 8 - 1
        row_above = pl.ds(jnp.maximum(start - 1, 0), 1)
        row_below = pl.ds(jnp.minimum(start + 8, rows - 1), 1)
        for p in range(RING):
            column = [field[p, here, :] for field in own]
            clear = jnp.ones((8, lanes), jnp.float32)
            red = green = blue = jnp.zeros((8, lanes), jnp.float32)
            for i, field in enumerate(own):
                s = column[i]
                k = i * RING + p
                above = jnp.where(first, up[k : k + 1, :], field[p, row_above, :])
                below = jnp.where(final, down[k : k + 1, :], field[p, row_below, :])
                above = jnp.where(sub == 0, above, pltpu.roll(s, 1, 0))
                below = jnp.where(sub == 7, below, pltpu.roll(s, 7, 0))
                dy = below - above
                if p > 0:
                    left = field[p - 1, here, :]
                else:
                    left = pltpu.roll(field[RING - 1, here, :], 1, 1)
                    left = jnp.where(lane == 0, 0.0, left)
                if p < RING - 1:
                    right = field[p + 1, here, :]
                else:
                    right = pltpu.roll(field[0, here, :], lanes - 1, 1)
                    right = jnp.where(lane == lanes - 1, 0.0, right)
                dx = right - left
                sloped = 0.168 * dy + 0.224 * dx
                squared = 0.25 * (dy * dy + dx * dx) + 1.0
                root = jnp.exp(0.5 * s)
                square = root * root
                fourth = square * square
                opacity = 1.0 - jnp.exp(-extinction * (square * root))
                weight = clear * opacity
                clear = clear - weight
                if 0 < i < count - 1:
                    dz = column[i + 1] - column[i - 1]
                    weight *= shade(dz, sloped, squared)
                dark = weight / (1.0 + fourth)
                bright = dark * fourth
                glow = weight * jnp.exp(-s * s)
                if 0 < i < count - 1:
                    red += bright
                    green += glow
                    blue += dark
                else:
                    base = 4 if i == 0 else 9
                    out[p, base, here, :] = bright
                    out[p, base + 1, here, :] = glow
                    out[p, base + 2, here, :] = dark
                    out[p, base + 3, here, :] = sloped
                    out[p, base + 4, here, :] = squared
            out[p, 0, here, :] = red
            out[p, 1, here, :] = green
            out[p, 2, here, :] = blue
            out[p, 3, here, :] = 1.0 - clear
        return carry

    lax.fori_loop(0, rows // 8, row_block, 0)


def shade(dz, sloped, squared):
    return 0.3 + jnp.abs(0.21 * dz + sloped) * lax.rsqrt(0.25 * (dz * dz) + squared)


def prepare(extinction, own, up, down):
    ring, rows, lanes = own[0].shape
    cells = ring * rows * lanes
    return pl.pallas_call(
        functools.partial(prepare_kernel, extinction, len(own)),
        in_specs=[pl.BlockSpec(memory_space=pltpu.VMEM)] * (len(own) + 2),
        out_specs=pl.BlockSpec(memory_space=pltpu.VMEM),
        out_shape=jax.ShapeDtypeStruct((ring, PARTS, rows, lanes), jnp.float32),
        compiler_params=params(32),
        cost_estimate=pl.CostEstimate(
            flops=len(own) * cells * 50, bytes_accessed=72 * cells, transcendentals=len(own) * cells * 5
        ),
        name="prepare",
    )(*own, up, down)


def slab_image(parts, second, before, inner, after):
    opening = shade(second - before, parts[7], parts[8])
    closing = shade(after - inner, parts[12], parts[13])
    return [parts[c] + opening * parts[4 + c] + closing * parts[9 + c] for c in range(3)] + [parts[3]]


def finish_kernel(places, parts, second, before, inner, after, out):
    for row in range(0, out.shape[1], 16):
        here = pl.ds(row, min(16, out.shape[1]))
        planes = [field[here] for field in (second, before, inner, after)]
        image = slab_image([parts[c, here] for c in range(PARTS)], *planes)
        for channel in range(4):
            out[channel, here] = image[channel]


def finish(places, slab):
    _, rows, lanes = slab[1].shape
    count = places.shape[0]
    whole = pl.BlockSpec((None, PARTS, rows, lanes), lambda i, place: (place[i], 0, 0, 0))
    plane = pl.BlockSpec((None, rows, lanes), lambda i, place: (place[i], 0, 0))
    cells = count * rows * lanes
    return pl.pallas_call(
        finish_kernel,
        grid_spec=pltpu.PrefetchScalarGridSpec(
            num_scalar_prefetch=1,
            grid=(count,),
            in_specs=[whole] + [plane] * 4,
            out_specs=[pl.BlockSpec((None, 4, rows, lanes), lambda i, place: (i, 0, 0, 0))],
        ),
        out_shape=[jax.ShapeDtypeStruct((count, 4, rows, lanes), jnp.float32)],
        compiler_params=params(12),
        cost_estimate=pl.CostEstimate(flops=cells * 30, bytes_accessed=cells * 88, transcendentals=cells * 2),
        name="finish",
    )(places, *slab)


def hop_kernel(near_own, received, own, out):
    for row in range(0, out.shape[1], 32):
        here = pl.ds(row, min(32, out.shape[1]))
        pair = (own[:, here], received[:, here])
        out[:, here] = over(*pair) if near_own else over(*pair[::-1])


def hop(received, chunks, number, near_own):
    shape = received.shape
    whole = pl.BlockSpec(shape, lambda i: (0, 0, 0))
    return pl.pallas_call(
        functools.partial(hop_kernel, near_own),
        grid=(1,),
        in_specs=[whole, pl.BlockSpec((None, *shape), lambda i: (number, 0, 0, 0))],
        out_specs=whole,
        out_shape=jax.ShapeDtypeStruct(shape, jnp.float32),
        compiler_params=params(8),
        cost_estimate=pl.CostEstimate(flops=received.size * 2, bytes_accessed=received.size * 12, transcendentals=0),
        name="hop_down" if near_own else "hop_up",
    )(received, chunks)


def merge_kernel(upper, own, left, right, *refs):
    *extras, out = refs
    groups, _, rows, quarter = out.shape
    selection = selection_matrix(quarter * groups, groups)
    step = min(rows, 32)
    for start in range(0, rows, step):
        here = pl.ds(start, step)
        image = over(over(left[:, here], own[:, here]), right[:, here])
        extra = extras[0][:, here] + extras[1][:, here] + extras[2][:, here]
        nearer = upper[0] > 0
        near = jnp.where(nearer, extra, image)
        far = jnp.where(nearer, image, extra)
        image = over(near, far)
        stacked = jnp.concatenate([thirds(image[channel]) for channel in range(4)], axis=0)
        sorted_rows = jnp.dot(stacked, selection, preferred_element_type=jnp.float32)
        for channel in range(4):
            for x in range(groups):
                out[x, channel, here] = sorted_rows[
                    channel * step : (channel + 1) * step, x * quarter : (x + 1) * quarter
                ]


def merge(upper, chunks, left, right, extras, groups):
    count, channels, rows, lanes = chunks.shape
    quarter = lanes // groups
    images = [left, right, *extras]

    def spec(shape):
        return pl.BlockSpec(shape, lambda i, upper: (0,) * len(shape))

    own = pl.BlockSpec((None, channels, rows, lanes), lambda i, upper: (count - 1, 0, 0, 0))
    return pl.pallas_call(
        merge_kernel,
        grid_spec=pltpu.PrefetchScalarGridSpec(
            num_scalar_prefetch=1,
            grid=(1,),
            in_specs=[own] + [spec(image.shape) for image in images],
            out_specs=spec((groups, channels, rows, quarter)),
        ),
        out_shape=jax.ShapeDtypeStruct((groups, channels, rows, quarter), jnp.float32),
        compiler_params=params(20),
        cost_estimate=pl.CostEstimate(
            flops=rows * lanes * 80, bytes_accessed=rows * lanes * 128, transcendentals=0
        ),
        name="merge",
    )(upper, chunks, *images)


def gather_ring(slab):
    depth = lax.axis_size("depth")
    index = lax.axis_index("depth")
    place = lax.rem(index, RING)
    last = depth - 1
    top = depth - RING
    half = RING // 2
    upper = place >= half
    send = functools.partial(lax.ppermute, axis_name="depth")

    (first,) = finish(lax.rem(place + half, RING)[None], slab)
    ups = [(i, i + 1) for i in range(last) if i % RING < half]
    downs = [(i + 1, i) for i in range(last) if (i + 1) % RING >= half]
    left = send(first[0], perm=ups)
    right = send(first[0], perm=downs)
    offsets = jnp.array([3, RING - 3, 2, RING - 2, 1, RING - 1, 0], jnp.int32)
    (chunks,) = finish(lax.rem(place + offsets, RING), slab)
    ups = [(i, i + 1) for i in range(last)]
    downs = [(i + 1, i) for i in range(last)]
    extras = []
    for step in range(3):
        distance = 3 - step
        forward = hop(left, chunks, 2 * step, False)
        left = send(forward, perm=ups)
        backward = hop(right, chunks, 2 * step + 1, True)
        right = send(backward, perm=downs)
        ends = (last, top + distance - 1), (0, RING - distance)
        extra = jnp.where(upper, forward, backward)
        if step == 1:
            detour = last - RING, RING
            extra = send(extra, perm=[(last, detour[0]), (0, detour[1])])
            ends = (detour[0], ends[0][1]), (detour[1], ends[1][1])
        extras.append(send(extra, perm=ends))

    groups = depth // RING
    quarters = merge(upper.astype(jnp.int32)[None], chunks, left, right, extras, groups)
    group = lax.div(index, RING)
    parts = []
    for shift in range(groups):
        part = lax.dynamic_index_in_dim(quarters, lax.rem(group + shift, groups), 0, keepdims=False)
        if shift:
            part = send(part, perm=[(i, (i + RING * shift) % depth) for i in range(depth)])
        parts.append(part)
    total = late = jnp.zeros_like(parts[0])
    for shift in range(groups - 1, -1, -1):
        turn = shift == group
        late = jnp.where(turn, total, late)
        total = jnp.where(turn, parts[shift], over(total, parts[shift]))
    return over(total, late)


def neighbours(axis):
    size = lax.axis_size(axis)
    ups = [(i, i + 1) for i in range(size - 1)]
    return ups, [(j, i) for i, j in ups]


def local(log_density):
    slices = log_density.shape[0]
    ups, downs = neighbours("depth")
    first, final, *outer_edges = split_classes(log_density, (0, slices - 1))
    before = lax.ppermute(final, "depth", ups)
    after = lax.ppermute(first, "depth", downs)
    inner = split_classes(log_density, range(1, slices - 1))
    inner, inner_edges = inner[: slices - 2], inner[slices - 2 :]
    edges = [outer_edges[0], *inner_edges, outer_edges[1]]
    slab = [first, *inner, final]
    ups, downs = neighbours("rows")
    up = lax.ppermute(jnp.concatenate([edge[1] for edge in edges]), "rows", ups)
    down = lax.ppermute(jnp.concatenate([edge[0] for edge in edges]), "rows", downs)
    parts = prepare(0.5 / (slices * lax.axis_size("depth")), slab, up, down)
    image = gather_ring([parts, inner[0], before, inner[-1], after])
    return image[:, :, None, :]


def solution(mesh):
    return jax.shard_map(
        local,
        mesh=mesh,
        in_specs=(P("depth", "rows", None),),
        out_specs=P(None, "rows", "depth", None),
        check_vma=False,
    )
```

```python
import functools

import jax
import jax.numpy as jnp
from jax import lax
from jax.experimental import pallas as pl
from jax.experimental.pallas import tpu as pltpu
from jax.sharding import PartitionSpec as P


RING = 8


def over(nearer, farther):
    return nearer + (1.0 - nearer[3:4]) * farther


def thirds(values):
    high = values.astype(jnp.bfloat16)
    rest = values - high.astype(jnp.float32)
    middle = rest.astype(jnp.bfloat16)
    low = (rest - middle.astype(jnp.float32)).astype(jnp.bfloat16)
    return jnp.concatenate([high, middle, low], axis=1)


def selection_matrix(width, classes):
    each = width // classes
    source = lax.broadcasted_iota(jnp.int32, (width, width), 0)
    column = lax.broadcasted_iota(jnp.int32, (width, width), 1)
    wanted = classes * (column & (each - 1)) + (column >> (each.bit_length() - 1))
    selection = jnp.where(source == wanted, 1.0, 0.0).astype(jnp.bfloat16)
    return jnp.concatenate([selection] * 3, axis=0)


def params(mebibytes):
    return pltpu.CompilerParams(vmem_limit_bytes=mebibytes * 2**20)


def split_kernel(*refs):
    *refs, selection = refs
    count = len(refs) // 3
    width = selection.shape[1]
    each = width // RING

    @pl.when(pl.program_id(0) == 0)
    def _():
        selection[...] = selection_matrix(width, RING)

    for field, out, edge in zip(refs[:count], refs[count : 2 * count], refs[2 * count :]):
        rows, columns = field.shape
        groups = range(columns // width)
        stacked = [thirds(field[:, b * width : (b + 1) * width]) for b in groups]
        sorted_rows = jnp.dot(
            jnp.concatenate(stacked, axis=0), selection[...], preferred_element_type=jnp.float32
        )
        blocks = [sorted_rows[b * rows : (b + 1) * rows] for b in groups]
        lane = lax.broadcasted_iota(jnp.int32, (rows, 4 * each), 1)
        lower, even = lane < 2 * each, (lane & each) == 0
        sides = {}
        for side in range(len(blocks) // 4):
            for half in range(RING // 4):
                tiles = [
                    block[:, half * 4 * each : (half + 1) * 4 * each]
                    for block in blocks[4 * side : 4 * side + 4]
                ]
                for a, b in ((0, 2), (1, 3)):
                    near, far = tiles[a], tiles[b]
                    tiles[a] = jnp.where(lower, near, pltpu.roll(far, 2 * each, 1))
                    tiles[b] = jnp.where(lower, pltpu.roll(near, 2 * each, 1), far)
                for a, b in ((0, 1), (2, 3)):
                    near, far = tiles[a], tiles[b]
                    tiles[a] = jnp.where(even, near, pltpu.roll(far, each, 1))
                    tiles[b] = jnp.where(even, pltpu.roll(near, 3 * each, 1), far)
                for k in range(4):
                    sides[4 * half + k, side] = tiles[k]
        for p in range(RING):
            values = jnp.concatenate([sides[p, side] for side in range(len(blocks) // 4)], axis=1)
            out[p] = values

            @pl.when(pl.program_id(0) == 0)
            def _(values=values, edge=edge, p=p):
                edge[0, p : p + 1] = values[:1]

            @pl.when(pl.program_id(0) == pl.num_programs(0) - 1)
            def _(values=values, edge=edge, p=p):
                edge[1, p : p + 1] = values[rows - 1 :]


def split_classes(field, chosen):
    _, rows, columns = field.shape
    step = min(rows, 64)
    lanes = columns // RING

    def source(i):
        return pl.BlockSpec((None, step, columns), lambda r: (i, r, 0))

    return pl.pallas_call(
        split_kernel,
        grid=(rows // step,),
        in_specs=[source(i) for i in chosen],
        out_specs=[pl.BlockSpec((RING, step, lanes), lambda r: (0, r, 0)) for _ in chosen]
        + [pl.BlockSpec((2, RING, lanes), lambda r: (0, 0, 0)) for _ in chosen],
        out_shape=[jax.ShapeDtypeStruct((RING, rows, lanes), jnp.float32) for _ in chosen]
        + [jax.ShapeDtypeStruct((2, RING, lanes), jnp.float32) for _ in chosen],
        scratch_shapes=[pltpu.VMEM((768, 256), jnp.bfloat16)],
        compiler_params=params(24),
        cost_estimate=pl.CostEstimate(
            flops=len(chosen) * rows * columns * 1536,
            bytes_accessed=len(chosen) * rows * columns * 8,
            transcendentals=0,
        ),
        name="split_classes",
    )(*[field] * len(chosen))


PARTS = 14


def prepare_kernel(extinction, count, *refs):
    own = refs[:count]
    up, down, out = refs[count:]
    _, rows, lanes = own[0].shape
    sub = lax.broadcasted_iota(jnp.int32, (8, lanes), 0)
    lane = lax.broadcasted_iota(jnp.int32, (8, lanes), 1)

    def row_block(block, carry):
        start = pl.multiple_of(block * 8, 8)
        here = pl.ds(start, 8)
        first = block == 0
        final = block == rows // 8 - 1
        row_above = pl.ds(jnp.maximum(start - 1, 0), 1)
        row_below = pl.ds(jnp.minimum(start + 8, rows - 1), 1)
        for p in range(RING):
            column = [field[p, here, :] for field in own]
            clear = jnp.ones((8, lanes), jnp.float32)
            red = green = blue = jnp.zeros((8, lanes), jnp.float32)
            for i, field in enumerate(own):
                s = column[i]
                k = i * RING + p
                above = jnp.where(first, up[k : k + 1, :], field[p, row_above, :])
                below = jnp.where(final, down[k : k + 1, :], field[p, row_below, :])
                above = jnp.where(sub == 0, above, pltpu.roll(s, 1, 0))
                below = jnp.where(sub == 7, below, pltpu.roll(s, 7, 0))
                dy = below - above
                if p > 0:
                    left = field[p - 1, here, :]
                else:
                    left = pltpu.roll(field[RING - 1, here, :], 1, 1)
                    left = jnp.where(lane == 0, 0.0, left)
                if p < RING - 1:
                    right = field[p + 1, here, :]
                else:
                    right = pltpu.roll(field[0, here, :], lanes - 1, 1)
                    right = jnp.where(lane == lanes - 1, 0.0, right)
                dx = right - left
                sloped = 0.168 * dy + 0.224 * dx
                squared = 0.25 * (dy * dy + dx * dx) + 1.0
                root = jnp.exp(0.5 * s)
                square = root * root
                fourth = square * square
                opacity = 1.0 - jnp.exp(-extinction * (square * root))
                weight = clear * opacity
                clear = clear - weight
                if 0 < i < count - 1:
                    dz = column[i + 1] - column[i - 1]
                    weight *= shade(dz, sloped, squared)
                dark = weight / (1.0 + fourth)
                bright = dark * fourth
                glow = weight * jnp.exp(-s * s)
                if 0 < i < count - 1:
                    red += bright
                    green += glow
                    blue += dark
                else:
                    base = 4 if i == 0 else 9
                    out[p, base, here, :] = bright
                    out[p, base + 1, here, :] = glow
                    out[p, base + 2, here, :] = dark
                    out[p, base + 3, here, :] = sloped
                    out[p, base + 4, here, :] = squared
            out[p, 0, here, :] = red
            out[p, 1, here, :] = green
            out[p, 2, here, :] = blue
            out[p, 3, here, :] = 1.0 - clear
        return carry

    lax.fori_loop(0, rows // 8, row_block, 0)


def shade(dz, sloped, squared):
    return 0.3 + jnp.abs(0.21 * dz + sloped) * lax.rsqrt(0.25 * (dz * dz) + squared)


def prepare(extinction, own, up, down):
    ring, rows, lanes = own[0].shape
    cells = ring * rows * lanes
    return pl.pallas_call(
        functools.partial(prepare_kernel, extinction, len(own)),
        in_specs=[pl.BlockSpec(memory_space=pltpu.VMEM)] * (len(own) + 2),
        out_specs=pl.BlockSpec(memory_space=pltpu.VMEM),
        out_shape=jax.ShapeDtypeStruct((ring, PARTS, rows, lanes), jnp.float32),
        compiler_params=params(32),
        cost_estimate=pl.CostEstimate(
            flops=len(own) * cells * 50, bytes_accessed=72 * cells, transcendentals=len(own) * cells * 5
        ),
        name="prepare",
    )(*own, up, down)


def slab_image(parts, second, before, inner, after):
    opening = shade(second - before, parts[7], parts[8])
    closing = shade(after - inner, parts[12], parts[13])
    return [parts[c] + opening * parts[4 + c] + closing * parts[9 + c] for c in range(3)] + [parts[3]]


def finish_kernel(places, parts, second, before, inner, after, out):
    for row in range(0, out.shape[1], 16):
        here = pl.ds(row, min(16, out.shape[1]))
        planes = [field[here] for field in (second, before, inner, after)]
        image = slab_image([parts[c, here] for c in range(PARTS)], *planes)
        for channel in range(4):
            out[channel, here] = image[channel]


def finish(places, slab):
    _, rows, lanes = slab[1].shape
    count = places.shape[0]
    whole = pl.BlockSpec((None, PARTS, rows, lanes), lambda i, place: (place[i], 0, 0, 0))
    plane = pl.BlockSpec((None, rows, lanes), lambda i, place: (place[i], 0, 0))
    cells = count * rows * lanes
    return pl.pallas_call(
        finish_kernel,
        grid_spec=pltpu.PrefetchScalarGridSpec(
            num_scalar_prefetch=1,
            grid=(count,),
            in_specs=[whole] + [plane] * 4,
            out_specs=[pl.BlockSpec((None, 4, rows, lanes), lambda i, place: (i, 0, 0, 0))],
        ),
        out_shape=[jax.ShapeDtypeStruct((count, 4, rows, lanes), jnp.float32)],
        compiler_params=params(12),
        cost_estimate=pl.CostEstimate(flops=cells * 30, bytes_accessed=cells * 88, transcendentals=cells * 2),
        name="finish",
    )(places, *slab)


def hop_kernel(near_own, received, own, out):
    for row in range(0, out.shape[1], 32):
        here = pl.ds(row, min(32, out.shape[1]))
        pair = (own[:, here], received[:, here])
        out[:, here] = over(*pair) if near_own else over(*pair[::-1])


def hop(received, chunks, number, near_own):
    shape = received.shape
    whole = pl.BlockSpec(shape, lambda i: (0, 0, 0))
    return pl.pallas_call(
        functools.partial(hop_kernel, near_own),
        grid=(1,),
        in_specs=[whole, pl.BlockSpec((None, *shape), lambda i: (number, 0, 0, 0))],
        out_specs=whole,
        out_shape=jax.ShapeDtypeStruct(shape, jnp.float32),
        compiler_params=params(8),
        cost_estimate=pl.CostEstimate(flops=received.size * 2, bytes_accessed=received.size * 12, transcendentals=0),
        name="hop_down" if near_own else "hop_up",
    )(received, chunks)


def merge_kernel(upper, own, left, right, *refs):
    *extras, out = refs
    groups, _, rows, quarter = out.shape
    selection = selection_matrix(quarter * groups, groups)
    step = min(rows, 32)
    for start in range(0, rows, step):
        here = pl.ds(start, step)
        image = over(over(left[:, here], own[:, here]), right[:, here])
        extra = extras[0][:, here] + extras[1][:, here] + extras[2][:, here]
        nearer = upper[0] > 0
        near = jnp.where(nearer, extra, image)
        far = jnp.where(nearer, image, extra)
        image = over(near, far)
        stacked = jnp.concatenate([thirds(image[channel]) for channel in range(4)], axis=0)
        sorted_rows = jnp.dot(stacked, selection, preferred_element_type=jnp.float32)
        for channel in range(4):
            for x in range(groups):
                out[x, channel, here] = sorted_rows[
                    channel * step : (channel + 1) * step, x * quarter : (x + 1) * quarter
                ]


def merge(upper, chunks, left, right, extras, groups):
    count, channels, rows, lanes = chunks.shape
    quarter = lanes // groups
    images = [left, right, *extras]

    def spec(shape):
        return pl.BlockSpec(shape, lambda i, upper: (0,) * len(shape))

    own = pl.BlockSpec((None, channels, rows, lanes), lambda i, upper: (count - 1, 0, 0, 0))
    return pl.pallas_call(
        merge_kernel,
        grid_spec=pltpu.PrefetchScalarGridSpec(
            num_scalar_prefetch=1,
            grid=(1,),
            in_specs=[own] + [spec(image.shape) for image in images],
            out_specs=spec((groups, channels, rows, quarter)),
        ),
        out_shape=jax.ShapeDtypeStruct((groups, channels, rows, quarter), jnp.float32),
        compiler_params=params(20),
        cost_estimate=pl.CostEstimate(
            flops=rows * lanes * 80, bytes_accessed=rows * lanes * 128, transcendentals=0
        ),
        name="merge",
    )(upper, chunks, *images)


def gather_ring(slab):
    depth = lax.axis_size("depth")
    index = lax.axis_index("depth")
    place = lax.rem(index, RING)
    last = depth - 1
    top = depth - RING
    half = RING // 2
    upper = place >= half
    send = functools.partial(lax.ppermute, axis_name="depth")

    offsets = jnp.array([half, 3, RING - 3, 2, RING - 2, 1, RING - 1, 0], jnp.int32)
    (chunks,) = finish(lax.rem(place + offsets, RING), slab)
    ups = [(i, i + 1) for i in range(last) if i % RING < half]
    downs = [(i + 1, i) for i in range(last) if (i + 1) % RING >= half]
    left = send(chunks[0], perm=ups)
    right = send(chunks[0], perm=downs)
    ups = [(i, i + 1) for i in range(last)]
    downs = [(i + 1, i) for i in range(last)]
    extras = []
    for step in range(3):
        distance = 3 - step
        ends = (last, top + distance - 1), (0, RING - distance)
        if step == 0:
            extras.append(send(jnp.where(upper, chunks[1], chunks[2]), perm=ends))
        forward = hop(left, chunks, 2 * step + 1, False)
        left = send(forward, perm=ups)
        backward = hop(right, chunks, 2 * step + 2, True)
        right = send(backward, perm=downs)
        if step:
            extras.append(send(jnp.where(upper, forward, backward), perm=ends))

    groups = depth // RING
    quarters = merge(upper.astype(jnp.int32)[None], chunks, left, right, extras, groups)
    rings = [[x * RING + z for x in range(groups)] for z in range(RING)]
    images = lax.all_to_all(quarters, "depth", 0, 0, axis_index_groups=rings, tiled=True)
    total = images[0]
    for x in range(1, groups):
        total = over(total, images[x])
    return total


def neighbours(axis):
    size = lax.axis_size(axis)
    ups = [(i, i + 1) for i in range(size - 1)]
    return ups, [(j, i) for i, j in ups]


def local(log_density):
    slices = log_density.shape[0]
    ups, downs = neighbours("depth")
    first, final, *outer_edges = split_classes(log_density, (0, slices - 1))
    before = lax.ppermute(final, "depth", ups)
    after = lax.ppermute(first, "depth", downs)
    inner = split_classes(log_density, range(1, slices - 1))
    inner, inner_edges = inner[: slices - 2], inner[slices - 2 :]
    edges = [outer_edges[0], *inner_edges, outer_edges[1]]
    slab = [first, *inner, final]
    ups, downs = neighbours("rows")
    up = lax.ppermute(jnp.concatenate([edge[1] for edge in edges]), "rows", ups)
    down = lax.ppermute(jnp.concatenate([edge[0] for edge in edges]), "rows", downs)
    parts = prepare(0.5 / (slices * lax.axis_size("depth")), slab, up, down)
    image = gather_ring([parts, inner[0], before, inner[-1], after])
    return image[:, :, None, :]


def solution(mesh):
    return jax.shard_map(
        local,
        mesh=mesh,
        in_specs=(P("depth", "rows", None),),
        out_specs=P(None, "rows", "depth", None),
        check_vma=False,
    )
```

```python
import functools

import jax
import jax.numpy as jnp
from jax import lax
from jax.experimental import pallas as pl
from jax.experimental.pallas import tpu as pltpu
from jax.sharding import PartitionSpec as P


RING = 8


def over(nearer, farther):
    return nearer + (1.0 - nearer[3:4]) * farther


def thirds(values):
    high = values.astype(jnp.bfloat16)
    rest = values - high.astype(jnp.float32)
    middle = rest.astype(jnp.bfloat16)
    low = (rest - middle.astype(jnp.float32)).astype(jnp.bfloat16)
    return jnp.concatenate([high, middle, low], axis=1)


def selection_matrix(width, classes):
    each = width // classes
    source = lax.broadcasted_iota(jnp.int32, (width, width), 0)
    column = lax.broadcasted_iota(jnp.int32, (width, width), 1)
    wanted = classes * (column & (each - 1)) + (column >> (each.bit_length() - 1))
    selection = jnp.where(source == wanted, 1.0, 0.0).astype(jnp.bfloat16)
    return jnp.concatenate([selection] * 3, axis=0)


def params(mebibytes):
    return pltpu.CompilerParams(vmem_limit_bytes=mebibytes * 2**20)


def split_kernel(*refs):
    *refs, selection = refs
    count = len(refs) // 3
    width = selection.shape[1]
    each = width // RING

    @pl.when(pl.program_id(0) == 0)
    def _():
        selection[...] = selection_matrix(width, RING)

    for field, out, edge in zip(refs[:count], refs[count : 2 * count], refs[2 * count :]):
        rows, columns = field.shape
        groups = range(columns // width)
        stacked = [thirds(field[:, b * width : (b + 1) * width]) for b in groups]
        sorted_rows = jnp.dot(
            jnp.concatenate(stacked, axis=0), selection[...], preferred_element_type=jnp.float32
        )
        blocks = [sorted_rows[b * rows : (b + 1) * rows] for b in groups]
        lane = lax.broadcasted_iota(jnp.int32, (rows, 4 * each), 1)
        lower, even = lane < 2 * each, (lane & each) == 0
        sides = {}
        for side in range(len(blocks) // 4):
            for half in range(RING // 4):
                tiles = [
                    block[:, half * 4 * each : (half + 1) * 4 * each]
                    for block in blocks[4 * side : 4 * side + 4]
                ]
                for a, b in ((0, 2), (1, 3)):
                    near, far = tiles[a], tiles[b]
                    tiles[a] = jnp.where(lower, near, pltpu.roll(far, 2 * each, 1))
                    tiles[b] = jnp.where(lower, pltpu.roll(near, 2 * each, 1), far)
                for a, b in ((0, 1), (2, 3)):
                    near, far = tiles[a], tiles[b]
                    tiles[a] = jnp.where(even, near, pltpu.roll(far, each, 1))
                    tiles[b] = jnp.where(even, pltpu.roll(near, 3 * each, 1), far)
                for k in range(4):
                    sides[4 * half + k, side] = tiles[k]
        for p in range(RING):
            values = jnp.concatenate([sides[p, side] for side in range(len(blocks) // 4)], axis=1)
            out[p] = values

            @pl.when(pl.program_id(0) == 0)
            def _(values=values, edge=edge, p=p):
                edge[0, p : p + 1] = values[:1]

            @pl.when(pl.program_id(0) == pl.num_programs(0) - 1)
            def _(values=values, edge=edge, p=p):
                edge[1, p : p + 1] = values[rows - 1 :]


def split_classes(field, chosen):
    _, rows, columns = field.shape
    step = min(rows, 64)
    lanes = columns // RING

    def source(i):
        return pl.BlockSpec((None, step, columns), lambda r: (i, r, 0))

    return pl.pallas_call(
        split_kernel,
        grid=(rows // step,),
        in_specs=[source(i) for i in chosen],
        out_specs=[pl.BlockSpec((RING, step, lanes), lambda r: (0, r, 0)) for _ in chosen]
        + [pl.BlockSpec((2, RING, lanes), lambda r: (0, 0, 0)) for _ in chosen],
        out_shape=[jax.ShapeDtypeStruct((RING, rows, lanes), jnp.float32) for _ in chosen]
        + [jax.ShapeDtypeStruct((2, RING, lanes), jnp.float32) for _ in chosen],
        scratch_shapes=[pltpu.VMEM((768, 256), jnp.bfloat16)],
        compiler_params=params(24),
        cost_estimate=pl.CostEstimate(
            flops=len(chosen) * rows * columns * 1536,
            bytes_accessed=len(chosen) * rows * columns * 8,
            transcendentals=0,
        ),
        name="split_classes",
    )(*[field] * len(chosen))


PARTS = 14


def prepare_kernel(extinction, count, *refs):
    own = refs[:count]
    up, down, out = refs[count:]
    _, rows, lanes = own[0].shape
    sub = lax.broadcasted_iota(jnp.int32, (8, lanes), 0)
    lane = lax.broadcasted_iota(jnp.int32, (8, lanes), 1)

    def row_block(block, carry):
        start = pl.multiple_of(block * 8, 8)
        here = pl.ds(start, 8)
        first = block == 0
        final = block == rows // 8 - 1
        row_above = pl.ds(jnp.maximum(start - 1, 0), 1)
        row_below = pl.ds(jnp.minimum(start + 8, rows - 1), 1)
        for p in range(RING):
            column = [field[p, here, :] for field in own]
            clear = jnp.ones((8, lanes), jnp.float32)
            red = green = blue = jnp.zeros((8, lanes), jnp.float32)
            for i, field in enumerate(own):
                s = column[i]
                k = i * RING + p
                above = jnp.where(first, up[k : k + 1, :], field[p, row_above, :])
                below = jnp.where(final, down[k : k + 1, :], field[p, row_below, :])
                above = jnp.where(sub == 0, above, pltpu.roll(s, 1, 0))
                below = jnp.where(sub == 7, below, pltpu.roll(s, 7, 0))
                dy = below - above
                if p > 0:
                    left = field[p - 1, here, :]
                else:
                    left = pltpu.roll(field[RING - 1, here, :], 1, 1)
                    left = jnp.where(lane == 0, 0.0, left)
                if p < RING - 1:
                    right = field[p + 1, here, :]
                else:
                    right = pltpu.roll(field[0, here, :], lanes - 1, 1)
                    right = jnp.where(lane == lanes - 1, 0.0, right)
                dx = right - left
                sloped = 0.168 * dy + 0.224 * dx
                squared = 0.25 * (dy * dy + dx * dx) + 1.0
                root = jnp.exp(0.5 * s)
                square = root * root
                fourth = square * square
                opacity = 1.0 - jnp.exp(-extinction * (square * root))
                weight = clear * opacity
                clear = clear - weight
                if 0 < i < count - 1:
                    dz = column[i + 1] - column[i - 1]
                    weight *= shade(dz, sloped, squared)
                dark = weight / (1.0 + fourth)
                bright = dark * fourth
                glow = weight * jnp.exp(-s * s)
                if 0 < i < count - 1:
                    red += bright
                    green += glow
                    blue += dark
                else:
                    base = 4 if i == 0 else 9
                    out[p, base, here, :] = bright
                    out[p, base + 1, here, :] = glow
                    out[p, base + 2, here, :] = dark
                    out[p, base + 3, here, :] = sloped
                    out[p, base + 4, here, :] = squared
            out[p, 0, here, :] = red
            out[p, 1, here, :] = green
            out[p, 2, here, :] = blue
            out[p, 3, here, :] = 1.0 - clear
        return carry

    lax.fori_loop(0, rows // 8, row_block, 0)


def shade(dz, sloped, squared):
    return 0.3 + jnp.abs(0.21 * dz + sloped) * lax.rsqrt(0.25 * (dz * dz) + squared)


def prepare(extinction, own, up, down):
    ring, rows, lanes = own[0].shape
    cells = ring * rows * lanes
    return pl.pallas_call(
        functools.partial(prepare_kernel, extinction, len(own)),
        in_specs=[pl.BlockSpec(memory_space=pltpu.VMEM)] * (len(own) + 2),
        out_specs=pl.BlockSpec(memory_space=pltpu.VMEM),
        out_shape=jax.ShapeDtypeStruct((ring, PARTS, rows, lanes), jnp.float32),
        compiler_params=params(32),
        cost_estimate=pl.CostEstimate(
            flops=len(own) * cells * 50, bytes_accessed=72 * cells, transcendentals=len(own) * cells * 5
        ),
        name="prepare",
    )(*own, up, down)


def slab_image(parts, second, before, inner, after):
    opening = shade(second - before, parts[7], parts[8])
    closing = shade(after - inner, parts[12], parts[13])
    return [parts[c] + opening * parts[4 + c] + closing * parts[9 + c] for c in range(3)] + [parts[3]]


def finish_kernel(places, parts, second, before, inner, after, out):
    for row in range(0, out.shape[1], 16):
        here = pl.ds(row, min(16, out.shape[1]))
        planes = [field[here] for field in (second, before, inner, after)]
        image = slab_image([parts[c, here] for c in range(PARTS)], *planes)
        for channel in range(4):
            out[channel, here] = image[channel]


def finish(places, slab):
    _, rows, lanes = slab[1].shape
    count = places.shape[0]
    whole = pl.BlockSpec((None, PARTS, rows, lanes), lambda i, place: (place[i], 0, 0, 0))
    plane = pl.BlockSpec((None, rows, lanes), lambda i, place: (place[i], 0, 0))
    cells = count * rows * lanes
    return pl.pallas_call(
        finish_kernel,
        grid_spec=pltpu.PrefetchScalarGridSpec(
            num_scalar_prefetch=1,
            grid=(count,),
            in_specs=[whole] + [plane] * 4,
            out_specs=[pl.BlockSpec((None, 4, rows, lanes), lambda i, place: (i, 0, 0, 0))],
        ),
        out_shape=[jax.ShapeDtypeStruct((count, 4, rows, lanes), jnp.float32)],
        compiler_params=params(12),
        cost_estimate=pl.CostEstimate(flops=cells * 30, bytes_accessed=cells * 88, transcendentals=cells * 2),
        name="finish",
    )(places, *slab)


def hop_kernel(near_own, received, own, out):
    for row in range(0, out.shape[1], 32):
        here = pl.ds(row, min(32, out.shape[1]))
        pair = (own[:, here], received[:, here])
        out[:, here] = over(*pair) if near_own else over(*pair[::-1])


def hop(received, chunks, number, near_own):
    shape = received.shape
    whole = pl.BlockSpec(shape, lambda i: (0, 0, 0))
    return pl.pallas_call(
        functools.partial(hop_kernel, near_own),
        grid=(1,),
        in_specs=[whole, pl.BlockSpec((None, *shape), lambda i: (number, 0, 0, 0))],
        out_specs=whole,
        out_shape=jax.ShapeDtypeStruct(shape, jnp.float32),
        compiler_params=params(8),
        cost_estimate=pl.CostEstimate(flops=received.size * 2, bytes_accessed=received.size * 12, transcendentals=0),
        name="hop_down" if near_own else "hop_up",
    )(received, chunks)


def merge_kernel(upper, own, left, right, *refs):
    *extras, out = refs
    groups, _, rows, quarter = out.shape
    selection = selection_matrix(quarter * groups, groups)
    step = min(rows, 32)
    for start in range(0, rows, step):
        here = pl.ds(start, step)
        image = over(over(left[:, here], own[:, here]), right[:, here])
        extra = extras[0][:, here] + extras[1][:, here] + extras[2][:, here]
        nearer = upper[0] > 0
        near = jnp.where(nearer, extra, image)
        far = jnp.where(nearer, image, extra)
        image = over(near, far)
        stacked = jnp.concatenate([thirds(image[channel]) for channel in range(4)], axis=0)
        sorted_rows = jnp.dot(stacked, selection, preferred_element_type=jnp.float32)
        for channel in range(4):
            for x in range(groups):
                out[x, channel, here] = sorted_rows[
                    channel * step : (channel + 1) * step, x * quarter : (x + 1) * quarter
                ]


def merge(upper, chunks, left, right, extras, groups):
    channels, rows, lanes = chunks.shape
    quarter = lanes // groups
    images = [left, right, *extras]

    def spec(shape):
        return pl.BlockSpec(shape, lambda i, upper: (0,) * len(shape))

    own = spec((channels, rows, lanes))
    return pl.pallas_call(
        merge_kernel,
        grid_spec=pltpu.PrefetchScalarGridSpec(
            num_scalar_prefetch=1,
            grid=(1,),
            in_specs=[own] + [spec(image.shape) for image in images],
            out_specs=spec((groups, channels, rows, quarter)),
        ),
        out_shape=jax.ShapeDtypeStruct((groups, channels, rows, quarter), jnp.float32),
        compiler_params=params(20),
        cost_estimate=pl.CostEstimate(
            flops=rows * lanes * 80, bytes_accessed=rows * lanes * 128, transcendentals=0
        ),
        name="merge",
    )(upper, chunks, *images)


def gather_ring(slab):
    depth = lax.axis_size("depth")
    index = lax.axis_index("depth")
    place = lax.rem(index, RING)
    last = depth - 1
    top = depth - RING
    half = RING // 2
    upper = place >= half
    send = functools.partial(lax.ppermute, axis_name="depth")

    offsets = jnp.array([half, 3, RING - 3, 2, RING - 2, 1, RING - 1, 0], jnp.int32)
    (chunks,) = finish(lax.rem(place + offsets, RING), slab)
    ups = [(i, i + 1) for i in range(last) if i % RING < half]
    downs = [(i + 1, i) for i in range(last) if (i + 1) % RING >= half]
    own = lax.optimization_barrier(chunks[RING - 1])
    left = send(chunks[0], perm=ups)
    right = send(chunks[0], perm=downs)
    ups = [(i, i + 1) for i in range(last)]
    downs = [(i + 1, i) for i in range(last)]
    extras = []
    for step in range(3):
        distance = 3 - step
        ends = (last, top + distance - 1), (0, RING - distance)
        if step == 0:
            extras.append(send(jnp.where(upper, chunks[1], chunks[2]), perm=ends))
        forward = hop(left, chunks, 2 * step + 1, False)
        left = send(forward, perm=ups)
        backward = hop(right, chunks, 2 * step + 2, True)
        right = send(backward, perm=downs)
        if step:
            extras.append(send(jnp.where(upper, forward, backward), perm=ends))

    groups = depth // RING
    quarters = merge(upper.astype(jnp.int32)[None], own, left, right, extras, groups)
    rings = [[x * RING + z for x in range(groups)] for z in range(RING)]
    images = lax.all_to_all(quarters, "depth", 0, 0, axis_index_groups=rings, tiled=True)
    total = images[0]
    for x in range(1, groups):
        total = over(total, images[x])
    return total


def neighbours(axis):
    size = lax.axis_size(axis)
    ups = [(i, i + 1) for i in range(size - 1)]
    return ups, [(j, i) for i, j in ups]


def local(log_density):
    slices = log_density.shape[0]
    ups, downs = neighbours("depth")
    log_density = pltpu.with_memory_space_constraint(log_density, pltpu.HBM)
    first, final, *outer_edges = split_classes(log_density, (0, slices - 1))
    before = lax.ppermute(final, "depth", ups)
    after = lax.ppermute(first, "depth", downs)
    inner = split_classes(log_density, range(1, slices - 1))
    inner, inner_edges = inner[: slices - 2], inner[slices - 2 :]
    edges = [outer_edges[0], *inner_edges, outer_edges[1]]
    slab = [first, *inner, final]
    ups, downs = neighbours("rows")
    up = lax.ppermute(jnp.concatenate([edge[1] for edge in edges]), "rows", ups)
    down = lax.ppermute(jnp.concatenate([edge[0] for edge in edges]), "rows", downs)
    parts = prepare(0.5 / (slices * lax.axis_size("depth")), slab, up, down)
    image = gather_ring([parts, inner[0], before, inner[-1], after])
    return image[:, :, None, :]


def solution(mesh):
    return jax.shard_map(
        local,
        mesh=mesh,
        in_specs=(P("depth", "rows", None),),
        out_specs=P(None, "rows", "depth", None),
        check_vma=False,
    )
```

```python
import functools

import jax
import jax.numpy as jnp
from jax import lax
from jax.experimental import pallas as pl
from jax.experimental.pallas import tpu as pltpu
from jax.sharding import PartitionSpec as P


RING = 8


def over(nearer, farther):
    return nearer + (1.0 - nearer[3:4]) * farther


def thirds(values):
    high = values.astype(jnp.bfloat16)
    rest = values - high.astype(jnp.float32)
    middle = rest.astype(jnp.bfloat16)
    low = (rest - middle.astype(jnp.float32)).astype(jnp.bfloat16)
    return jnp.concatenate([high, middle, low], axis=1)


def selection_matrix(width, classes):
    each = width // classes
    source = lax.broadcasted_iota(jnp.int32, (width, width), 0)
    column = lax.broadcasted_iota(jnp.int32, (width, width), 1)
    wanted = classes * (column & (each - 1)) + (column >> (each.bit_length() - 1))
    selection = jnp.where(source == wanted, 1.0, 0.0).astype(jnp.bfloat16)
    return jnp.concatenate([selection] * 3, axis=0)


def params(mebibytes):
    return pltpu.CompilerParams(vmem_limit_bytes=mebibytes * 2**20)


def split_kernel(*refs):
    *refs, selection = refs
    count = len(refs) // 3
    width = selection.shape[1]
    each = width // RING

    @pl.when(pl.program_id(0) == 0)
    def _():
        selection[...] = selection_matrix(width, RING)

    for field, out, edge in zip(refs[:count], refs[count : 2 * count], refs[2 * count :]):
        rows, columns = field.shape
        groups = range(columns // width)
        stacked = [thirds(field[:, b * width : (b + 1) * width]) for b in groups]
        sorted_rows = jnp.dot(
            jnp.concatenate(stacked, axis=0), selection[...], preferred_element_type=jnp.float32
        )
        blocks = [sorted_rows[b * rows : (b + 1) * rows] for b in groups]
        lane = lax.broadcasted_iota(jnp.int32, (rows, 4 * each), 1)
        lower, even = lane < 2 * each, (lane & each) == 0
        sides = {}
        for side in range(len(blocks) // 4):
            for half in range(RING // 4):
                tiles = [
                    block[:, half * 4 * each : (half + 1) * 4 * each]
                    for block in blocks[4 * side : 4 * side + 4]
                ]
                for a, b in ((0, 2), (1, 3)):
                    near, far = tiles[a], tiles[b]
                    tiles[a] = jnp.where(lower, near, pltpu.roll(far, 2 * each, 1))
                    tiles[b] = jnp.where(lower, pltpu.roll(near, 2 * each, 1), far)
                for a, b in ((0, 1), (2, 3)):
                    near, far = tiles[a], tiles[b]
                    tiles[a] = jnp.where(even, near, pltpu.roll(far, each, 1))
                    tiles[b] = jnp.where(even, pltpu.roll(near, 3 * each, 1), far)
                for k in range(4):
                    sides[4 * half + k, side] = tiles[k]
        for p in range(RING):
            values = jnp.concatenate([sides[p, side] for side in range(len(blocks) // 4)], axis=1)
            out[p] = values

            @pl.when(pl.program_id(0) == 0)
            def _(values=values, edge=edge, p=p):
                edge[0, p : p + 1] = values[:1]

            @pl.when(pl.program_id(0) == pl.num_programs(0) - 1)
            def _(values=values, edge=edge, p=p):
                edge[1, p : p + 1] = values[rows - 1 :]


def split_classes(field, chosen):
    _, rows, columns = field.shape
    step = min(rows, 64)
    lanes = columns // RING

    def source(i):
        return pl.BlockSpec((None, step, columns), lambda r: (i, r, 0))

    return pl.pallas_call(
        split_kernel,
        grid=(rows // step,),
        in_specs=[source(i) for i in chosen],
        out_specs=[pl.BlockSpec((RING, step, lanes), lambda r: (0, r, 0)) for _ in chosen]
        + [pl.BlockSpec((2, RING, lanes), lambda r: (0, 0, 0)) for _ in chosen],
        out_shape=[jax.ShapeDtypeStruct((RING, rows, lanes), jnp.float32) for _ in chosen]
        + [jax.ShapeDtypeStruct((2, RING, lanes), jnp.float32) for _ in chosen],
        scratch_shapes=[pltpu.VMEM((768, 256), jnp.bfloat16)],
        compiler_params=params(24),
        cost_estimate=pl.CostEstimate(
            flops=len(chosen) * rows * columns * 1536,
            bytes_accessed=len(chosen) * rows * columns * 8,
            transcendentals=0,
        ),
        name="split_classes",
    )(*[field] * len(chosen))


PARTS = 14


def prepare_kernel(extinction, count, *refs):
    own = refs[:count]
    up, down, out = refs[count:]
    _, rows, lanes = own[0].shape
    sub = lax.broadcasted_iota(jnp.int32, (8, lanes), 0)
    lane = lax.broadcasted_iota(jnp.int32, (8, lanes), 1)

    def row_block(block, carry):
        start = pl.multiple_of(block * 8, 8)
        here = pl.ds(start, 8)
        first = block == 0
        final = block == rows // 8 - 1
        row_above = pl.ds(jnp.maximum(start - 1, 0), 1)
        row_below = pl.ds(jnp.minimum(start + 8, rows - 1), 1)
        for p in range(RING):
            column = [field[p, here, :] for field in own]
            clear = jnp.ones((8, lanes), jnp.float32)
            red = green = blue = jnp.zeros((8, lanes), jnp.float32)
            for i, field in enumerate(own):
                s = column[i]
                k = i * RING + p
                above = jnp.where(first, up[k : k + 1, :], field[p, row_above, :])
                below = jnp.where(final, down[k : k + 1, :], field[p, row_below, :])
                above = jnp.where(sub == 0, above, pltpu.roll(s, 1, 0))
                below = jnp.where(sub == 7, below, pltpu.roll(s, 7, 0))
                dy = below - above
                if p > 0:
                    left = field[p - 1, here, :]
                else:
                    left = pltpu.roll(field[RING - 1, here, :], 1, 1)
                    left = jnp.where(lane == 0, 0.0, left)
                if p < RING - 1:
                    right = field[p + 1, here, :]
                else:
                    right = pltpu.roll(field[0, here, :], lanes - 1, 1)
                    right = jnp.where(lane == lanes - 1, 0.0, right)
                dx = right - left
                sloped = 0.168 * dy + 0.224 * dx
                squared = 0.25 * (dy * dy + dx * dx) + 1.0
                root = jnp.exp(0.5 * s)
                square = root * root
                fourth = square * square
                opacity = 1.0 - jnp.exp(-extinction * (square * root))
                weight = clear * opacity
                clear = clear - weight
                if 0 < i < count - 1:
                    dz = column[i + 1] - column[i - 1]
                    weight *= shade(dz, sloped, squared)
                dark = weight / (1.0 + fourth)
                bright = dark * fourth
                glow = weight * jnp.exp(-s * s)
                if 0 < i < count - 1:
                    red += bright
                    green += glow
                    blue += dark
                else:
                    base = 4 if i == 0 else 9
                    out[p, base, here, :] = bright
                    out[p, base + 1, here, :] = glow
                    out[p, base + 2, here, :] = dark
                    out[p, base + 3, here, :] = sloped
                    out[p, base + 4, here, :] = squared
            out[p, 0, here, :] = red
            out[p, 1, here, :] = green
            out[p, 2, here, :] = blue
            out[p, 3, here, :] = 1.0 - clear
        return carry

    lax.fori_loop(0, rows // 8, row_block, 0)


def shade(dz, sloped, squared):
    return 0.3 + jnp.abs(0.21 * dz + sloped) * lax.rsqrt(0.25 * (dz * dz) + squared)


def prepare(extinction, own, up, down):
    ring, rows, lanes = own[0].shape
    cells = ring * rows * lanes
    return pl.pallas_call(
        functools.partial(prepare_kernel, extinction, len(own)),
        in_specs=[pl.BlockSpec(memory_space=pltpu.VMEM)] * (len(own) + 2),
        out_specs=pl.BlockSpec(memory_space=pltpu.VMEM),
        out_shape=jax.ShapeDtypeStruct((ring, PARTS, rows, lanes), jnp.float32),
        compiler_params=params(32),
        cost_estimate=pl.CostEstimate(
            flops=len(own) * cells * 50, bytes_accessed=72 * cells, transcendentals=len(own) * cells * 5
        ),
        name="prepare",
    )(*own, up, down)


def slab_image(parts, second, before, inner, after):
    opening = shade(second - before, parts[7], parts[8])
    closing = shade(after - inner, parts[12], parts[13])
    return [parts[c] + opening * parts[4 + c] + closing * parts[9 + c] for c in range(3)] + [parts[3]]


def finish_kernel(places, parts, second, before, inner, after, out):
    for row in range(0, out.shape[1], 16):
        here = pl.ds(row, min(16, out.shape[1]))
        planes = [field[here] for field in (second, before, inner, after)]
        image = slab_image([parts[c, here] for c in range(PARTS)], *planes)
        for channel in range(4):
            out[channel, here] = image[channel]


def finish(places, slab):
    _, rows, lanes = slab[1].shape
    count = places.shape[0]
    whole = pl.BlockSpec((None, PARTS, rows, lanes), lambda i, place: (place[i], 0, 0, 0))
    plane = pl.BlockSpec((None, rows, lanes), lambda i, place: (place[i], 0, 0))
    cells = count * rows * lanes
    return pl.pallas_call(
        finish_kernel,
        grid_spec=pltpu.PrefetchScalarGridSpec(
            num_scalar_prefetch=1,
            grid=(count,),
            in_specs=[whole] + [plane] * 4,
            out_specs=[pl.BlockSpec((None, 4, rows, lanes), lambda i, place: (i, 0, 0, 0))],
        ),
        out_shape=[jax.ShapeDtypeStruct((count, 4, rows, lanes), jnp.float32)],
        compiler_params=params(12),
        cost_estimate=pl.CostEstimate(flops=cells * 30, bytes_accessed=cells * 88, transcendentals=cells * 2),
        name="finish",
    )(places, *slab)


def hop_kernel(near_own, received, own, out):
    for row in range(0, out.shape[1], 32):
        here = pl.ds(row, min(32, out.shape[1]))
        pair = (own[:, here], received[:, here])
        out[:, here] = over(*pair) if near_own else over(*pair[::-1])


def hop(received, chunks, number, near_own):
    shape = received.shape
    whole = pl.BlockSpec(shape, lambda i: (0, 0, 0))
    return pl.pallas_call(
        functools.partial(hop_kernel, near_own),
        grid=(1,),
        in_specs=[whole, pl.BlockSpec((None, *shape), lambda i: (number, 0, 0, 0))],
        out_specs=whole,
        out_shape=jax.ShapeDtypeStruct(shape, jnp.float32),
        compiler_params=params(8),
        cost_estimate=pl.CostEstimate(flops=received.size * 2, bytes_accessed=received.size * 12, transcendentals=0),
        name="hop_down" if near_own else "hop_up",
    )(received, chunks)


def merge_kernel(upper, own, left, right, *refs):
    *extras, out = refs
    groups, _, rows, quarter = out.shape
    selection = selection_matrix(quarter * groups, groups)
    step = min(rows, 32)
    for start in range(0, rows, step):
        here = pl.ds(start, step)
        image = over(over(left[:, here], own[:, here]), right[:, here])
        extra = extras[0][:, here] + extras[1][:, here] + extras[2][:, here]
        nearer = upper[0] > 0
        near = jnp.where(nearer, extra, image)
        far = jnp.where(nearer, image, extra)
        image = over(near, far)
        stacked = jnp.concatenate([thirds(image[channel]) for channel in range(4)], axis=0)
        sorted_rows = jnp.dot(stacked, selection, preferred_element_type=jnp.float32)
        for channel in range(4):
            for x in range(groups):
                out[x, channel, here] = sorted_rows[
                    channel * step : (channel + 1) * step, x * quarter : (x + 1) * quarter
                ]


def merge(upper, chunks, left, right, extras, groups):
    channels, rows, lanes = chunks.shape
    quarter = lanes // groups
    images = [left, right, *extras]

    def spec(shape):
        return pl.BlockSpec(shape, lambda i, upper: (0,) * len(shape))

    own = spec((channels, rows, lanes))
    return pl.pallas_call(
        merge_kernel,
        grid_spec=pltpu.PrefetchScalarGridSpec(
            num_scalar_prefetch=1,
            grid=(1,),
            in_specs=[own] + [spec(image.shape) for image in images],
            out_specs=spec((groups, channels, rows, quarter)),
        ),
        out_shape=jax.ShapeDtypeStruct((groups, channels, rows, quarter), jnp.float32),
        compiler_params=params(20),
        cost_estimate=pl.CostEstimate(
            flops=rows * lanes * 80, bytes_accessed=rows * lanes * 128, transcendentals=0
        ),
        name="merge",
    )(upper, chunks, *images)


def fold_kernel(images, out):
    rows = out.shape[1]
    step = min(rows, 32)
    for start in range(0, rows, step):
        here = pl.ds(start, step)
        total = images[0, :, here]
        for x in range(1, images.shape[0]):
            total = over(total, images[x, :, here])
        out[:, here] = total


def fold(images):
    shape = images.shape[1:]
    return pl.pallas_call(
        fold_kernel,
        grid=(1,),
        in_specs=[pl.BlockSpec(images.shape, lambda i: (0, 0, 0, 0))],
        out_specs=pl.BlockSpec(shape, lambda i: (0, 0, 0)),
        out_shape=jax.ShapeDtypeStruct(shape, jnp.float32),
        compiler_params=params(12),
        name="fold",
    )(images)


def gather_ring(slab):
    depth = lax.axis_size("depth")
    index = lax.axis_index("depth")
    place = lax.rem(index, RING)
    last = depth - 1
    top = depth - RING
    half = RING // 2
    upper = place >= half
    send = functools.partial(lax.ppermute, axis_name="depth")

    offsets = jnp.array([half, 3, RING - 3, 2, RING - 2, 1, RING - 1, 0], jnp.int32)
    (chunks,) = finish(lax.rem(place + offsets, RING), slab)
    ups = [(i, i + 1) for i in range(last) if i % RING < half]
    downs = [(i + 1, i) for i in range(last) if (i + 1) % RING >= half]
    own = lax.optimization_barrier(chunks[RING - 1])
    left = send(chunks[0], perm=ups)
    right = send(chunks[0], perm=downs)
    ups = [(i, i + 1) for i in range(last)]
    downs = [(i + 1, i) for i in range(last)]
    extras = []
    for step in range(3):
        distance = 3 - step
        ends = (last, top + distance - 1), (0, RING - distance)
        if step == 0:
            extras.append(send(jnp.where(upper, chunks[1], chunks[2]), perm=ends))
        forward = hop(left, chunks, 2 * step + 1, False)
        left = send(forward, perm=ups)
        backward = hop(right, chunks, 2 * step + 2, True)
        right = send(backward, perm=downs)
        if step:
            extras.append(send(jnp.where(upper, forward, backward), perm=ends))

    groups = depth // RING
    quarters = merge(upper.astype(jnp.int32)[None], own, left, right, extras, groups)
    rings = [[x * RING + z for x in range(groups)] for z in range(RING)]
    images = lax.all_to_all(quarters, "depth", 0, 0, axis_index_groups=rings, tiled=True)
    return fold(images)


def neighbours(axis):
    size = lax.axis_size(axis)
    ups = [(i, i + 1) for i in range(size - 1)]
    return ups, [(j, i) for i, j in ups]


def local(log_density):
    slices = log_density.shape[0]
    ups, downs = neighbours("depth")
    log_density = pltpu.with_memory_space_constraint(log_density, pltpu.HBM)
    first, final, *outer_edges = split_classes(log_density, (0, slices - 1))
    before = lax.ppermute(final, "depth", ups)
    after = lax.ppermute(first, "depth", downs)
    inner = split_classes(log_density, range(1, slices - 1))
    inner, inner_edges = inner[: slices - 2], inner[slices - 2 :]
    edges = [outer_edges[0], *inner_edges, outer_edges[1]]
    slab = [first, *inner, final]
    ups, downs = neighbours("rows")
    up = lax.ppermute(jnp.concatenate([edge[1] for edge in edges]), "rows", ups)
    down = lax.ppermute(jnp.concatenate([edge[0] for edge in edges]), "rows", downs)
    parts = prepare(0.5 / (slices * lax.axis_size("depth")), slab, up, down)
    image = gather_ring([parts, inner[0], before, inner[-1], after])
    return image[:, :, None, :]


def solution(mesh):
    return jax.shard_map(
        local,
        mesh=mesh,
        in_specs=(P("depth", "rows", None),),
        out_specs=P(None, "rows", "depth", None),
        check_vma=False,
    )
```
